32 devices in a mesh: dom: 8 (over y, x, core), grp: 4 (over z).
Axes of the slice: x: 2, y: 2, z: 4, core: 2. Of those that a mesh axis runs over, the one named last changes fastest.
Arguments:
- embeddings: float32 [4, 4096, 512], P('grp', 'dom'), may hold values from -18 to 18
- ada_state: float32 [4, 4096], P('grp', 'dom'), may hold values from 0.05 to 1
- relations: float32 [4, 512, 512], replicated, may hold values from -0.25 to 0.25
- plan: int32 [2], replicated, may hold values from 1 to 7, as said below
- src_rows: int32 [4, 8, 2, 512], P('grp', 'dom'), may hold values from 0 to 511
- dst_rows: int32 [4, 8, 2, 512], P('grp', 'dom'), may hold values from 0 to 511
- rel_ids: int32 [4, 8, 2, 512], P('grp', 'dom'), may hold values from 0 to 3
Outputs:
- new_embeddings: float32 [4, 4096, 512], P('grp', 'dom')
- new_state: float32 [4, 4096], P('grp', 'dom')
- rel_grad: float32 [4, 512, 512], replicated
- mean_loss: float32 [], replicated
The draws below stay inside these ranges and needn't reach their ends.
Inputs may be any that keep to these rules, and one draw needn't show every extreme that they name: `plan`: the 2 values are distinct; 7 occurs.
All inputs are finite; a program needn't handle non-finite values.
Results may differ from the reference program's by a relative error of at most 0.02.
Values may be sent and summed in bfloat16 or wider, within the bound.
No kernel may reach another device: no remote copies, remote signals or barrier semaphores. Data moves between devices by JAX's collectives and lax.ppermute only.
A program may use at most 64 MiB of HBM per device.

```python
import math
import jax
import jax.numpy as jnp
from jax import lax

D = 512
ROWS = 512
EDGES = 512
NREL = 4
ROUNDS = 2
ENT = 4096
N_DOM = 8
N_GRP = 4


def draw_embeddings(key, part):
    key_base, key_scale = jax.random.split(key, 2)
    normals = jnp.clip(jax.random.normal(key_base, (N_GRP, ENT, D), jnp.float32), -6.0, 6.0)
    row_scale = 0.25 * jnp.exp(jax.random.uniform(key_scale, (N_GRP, ENT, 1), jnp.float32, -0.7, 0.7))
    return normals * row_scale


def draw_plan(key, part):
    key_pick, key_order = jax.random.split(key)
    others = jax.random.permutation(key_pick, N_DOM - 2)[:ROUNDS - 1].astype(jnp.int32) + 1
    masks_all = jnp.concatenate([jnp.array([N_DOM - 1], jnp.int32), others])
    shuffle = jax.random.permutation(key_order, ROUNDS)
    return masks_all[shuffle]


def touch_ends(entries, own_key, low, largest):
    longest = entries.shape.index(max(entries.shape))
    spots = []
    for shift in (0, 1):
        where = [jax.random.randint(jax.random.fold_in(own_key, axis), (), 0, length) for axis, length in enumerate(entries.shape)]
        where[longest] = (where[longest] + shift) % entries.shape[longest]
        spots.append(tuple(where))
    return entries.at[spots[0]].set(low).at[spots[1]].set(largest)


def shard_levels(own_key, extent, cuts, least, high):
    level = 1.0
    for axis_at, blocks in cuts:
        draws = jax.random.uniform(jax.random.fold_in(jax.random.fold_in(own_key, 6), axis_at), (blocks,), jnp.float32, least / len(cuts), high / len(cuts))
        level = level * jnp.repeat(jnp.exp(draws), extent[axis_at] // blocks).reshape((-1,) + (1,) * (len(extent) - 1 - axis_at))
    return level


def noise(key, dims, deviation, bound, held_as=jnp.bfloat16):
    values = jax.random.normal(key, dims, jnp.float32) * deviation
    return jnp.minimum(jnp.maximum(values, -bound), bound).astype(held_as)


def setup_inputs(seed: int = 0) -> dict:
    splits = jax.random.split(jax.random.key(seed), 8)
    return {
        "embeddings": draw_embeddings(jax.random.fold_in(splits[7], 71), 0),
        "ada_state": jnp.clip(jnp.exp(math.log(1.0) - 2.9957323 * jax.random.uniform(splits[1], (N_GRP, ENT), jnp.float32) ** shard_levels(splits[1], (N_GRP, ENT), ((0, 4), (1, 8)), -0.2, 0.2)), 0.05, 1.0),
        "relations": noise(splits[2], (NREL, D, D), D ** -0.5, 0.25, jnp.float32),
        "plan": draw_plan(jax.random.fold_in(splits[7], 71), 0),
        "src_rows": touch_ends(jax.random.randint(splits[4], (N_GRP, N_DOM, ROUNDS, EDGES), 0, ROWS), jax.random.fold_in(splits[4], 1), 0, ROWS - 1).astype(jnp.int32),
        "dst_rows": touch_ends(jax.random.randint(splits[5], (N_GRP, N_DOM, ROUNDS, EDGES), 0, ROWS), jax.random.fold_in(splits[5], 1), 0, ROWS - 1).astype(jnp.int32),
        "rel_ids": touch_ends(jax.random.randint(splits[6], (N_GRP, N_DOM, ROUNDS, EDGES), 0, NREL), jax.random.fold_in(splits[6], 1), 0, NREL - 1).astype(jnp.int32),
    }


LEARN_RATE = 0.1
EPSILON = 1e-08

def project_queries(own_rows, src_idx, rel_idx, rel_b):
    src_b = own_rows[src_idx].astype(jnp.bfloat16)
    projected = jnp.einsum('ed,kdf->kef', src_b.astype(jnp.float32), rel_b.astype(jnp.float32))
    onehot = (rel_idx[None, :] == jnp.arange(NREL, dtype=jnp.int32)[:, None]).astype(jnp.float32)
    queries = lax.optimization_barrier(jnp.sum(onehot[:, :, None] * projected, axis=0)).astype(jnp.bfloat16)
    return (src_b, queries, onehot)

def score_block(queries, block_b, dst_idx):
    scores = jnp.dot(queries, block_b.T, preferred_element_type=jnp.float32)
    row_max = lax.optimization_barrier(jnp.max(scores, axis=1, keepdims=True))
    exp_scores = jnp.exp(scores - row_max)
    row_total = lax.optimization_barrier(jnp.sum(exp_scores, axis=1, keepdims=True))
    targets = (dst_idx[:, None] == jnp.arange(block_b.shape[0], dtype=jnp.int32)[None, :]).astype(jnp.float32)
    edge_loss = row_max[:, 0] + jnp.log(row_total[:, 0]) - lax.optimization_barrier(jnp.sum(scores * targets, axis=1))
    deltas = (exp_scores / row_total - targets).astype(jnp.bfloat16)
    dquery = jnp.dot(deltas, block_b, preferred_element_type=jnp.float32).astype(jnp.bfloat16)
    dblock = jnp.dot(deltas.T, queries, preferred_element_type=jnp.float32).astype(jnp.bfloat16)
    return (jnp.sum(edge_loss), dquery, dblock)

def apply_back(dquery, src_b, onehot, rel_b, src_idx):
    back_proj = jnp.einsum('ef,kdf->ked', dquery.astype(jnp.float32), rel_b.astype(jnp.float32))
    src_grad = lax.optimization_barrier(jnp.sum(onehot[:, :, None] * back_proj, axis=0))
    gradient = jnp.zeros((ROWS, src_grad.shape[1]), src_grad.dtype).at[src_idx].add(src_grad)
    masked = onehot[:, :, None] * dquery.astype(jnp.float32)
    rel_part = jnp.einsum('ed,kef->kdf', src_b.astype(jnp.float32), masked)
    return (gradient, rel_part)

def adagrad(own_rows, row_state, gradient):
    new_state = row_state + lax.optimization_barrier(jnp.mean(gradient * gradient, axis=-1))
    new_rows = own_rows - LEARN_RATE * gradient / (jnp.sqrt(new_state)[:, None] + EPSILON)
    return (new_rows, new_state)

def reference(embeddings, ada_state, relations, plan, src_rows, dst_rows, rel_ids):
    rel_b = relations.astype(jnp.bfloat16)

    def one_group(group_args):
        emb_rows, state_rows, src_all, dst_all, rel_all = group_args
        blocks = emb_rows.reshape(N_DOM, ROWS, D)
        row_state = state_rows.reshape(N_DOM, ROWS)
        loss_sum = jnp.zeros((), jnp.float32)
        rel_sum = jnp.zeros((NREL, D, D), jnp.float32)
        for round_no in range(ROUNDS):
            partner = jnp.bitwise_xor(jnp.arange(N_DOM, dtype=jnp.int32), plan[round_no])
            src_b, queries, onehot = jax.vmap(project_queries, (0, 0, 0, None))(blocks, src_all[:, round_no], rel_all[:, round_no], rel_b)
            part_b = blocks.astype(jnp.bfloat16)[partner]
            edge_loss, dquery, dblock = jax.vmap(score_block)(queries, part_b, dst_all[:, round_no])
            gradient, rel_part = jax.vmap(apply_back, (0, 0, 0, None, 0))(dquery, src_b, onehot, rel_b, src_all[:, round_no])
            gradient = gradient + dblock[partner].astype(jnp.float32)
            blocks, row_state = jax.vmap(adagrad)(blocks, row_state, gradient)
            loss_sum = loss_sum + jnp.sum(edge_loss)
            rel_sum = rel_sum + lax.optimization_barrier(jnp.sum(rel_part, axis=0))
        return (blocks.reshape(ENT, D), row_state.reshape(ENT), rel_sum, loss_sum)
    results = lax.map(one_group, (embeddings, ada_state, src_rows, dst_rows, rel_ids))
    rel_grad = lax.optimization_barrier(jnp.sum(results[2], axis=0))
    mean_loss = jnp.sum(results[3]) / (N_GRP * N_DOM * ROUNDS * EDGES)
    return (results[0], results[1], rel_grad, mean_loss)
```

```python
import jax
import jax.numpy as jnp
from jax import lax
from jax.sharding import PartitionSpec as P

EDGES = 512
ROUNDS = 2


LEARN_RATE = 0.1
EPSILON = 1e-08
DIGIT = 3
RADIX = 128


def xor_route(axis, mask):
    return [(low, low ^ mask) for low in range(lax.axis_size(axis))]


def exchange(block, axis, mask):
    bits = lax.axis_size(axis).bit_length() - 1
    done = 0
    while done < bits:
        width = min(DIGIT, bits - done)
        digit = jnp.bitwise_and(jnp.right_shift(mask, done), (1 << width) - 1)
        branches = [lambda x: x]
        for value in range(1, 1 << width):
            route = xor_route(axis, value << done)
            branches.append(lambda x, route=route: lax.ppermute(x, axis, route))
        block = lax.switch(digit, branches, block)
        done += width
    return block


def project(src_b, rel_idx, rel_b):
    projected = jnp.einsum("ed,kdf->kef", src_b, rel_b, preferred_element_type=jnp.float32)
    onehot = (rel_idx[None, :] == jnp.arange(rel_b.shape[0], dtype=jnp.int32)[:, None]).astype(
        jnp.float32
    )
    return jnp.sum(onehot[:, :, None] * projected, axis=0).astype(jnp.bfloat16), onehot


def score(queries, block_b, dst_idx):
    scores = jnp.dot(queries, block_b.T, preferred_element_type=jnp.float32)
    row_max = jnp.max(scores, axis=1, keepdims=True)
    exp_scores = jnp.exp(scores - row_max)
    row_total = jnp.sum(exp_scores, axis=1, keepdims=True)
    targets = (dst_idx[:, None] == jnp.arange(block_b.shape[0], dtype=jnp.int32)[None, :]).astype(
        jnp.float32
    )
    edge_loss = row_max[:, 0] + jnp.log(row_total[:, 0]) - jnp.sum(scores * targets, axis=1)
    deltas = (exp_scores / row_total - targets).astype(jnp.bfloat16)
    return jnp.sum(edge_loss), deltas


def encode(idx, width):
    rows = []
    for part in idx:
        rows += [part // RADIX, part % RADIX]
    rows = jnp.stack(rows).astype(jnp.bfloat16)
    return jnp.pad(rows, ((0, 16 - rows.shape[0]), (0, 0)))


def decode(rows):
    rows = rows.astype(jnp.float32).astype(jnp.int32)
    return [rows[2 * n] * RADIX + rows[2 * n + 1] for n in range(3)]


def pieces(total):
    high = total.astype(jnp.bfloat16)
    rest = total - high.astype(jnp.float32)
    mid = rest.astype(jnp.bfloat16)
    low = (rest - mid.astype(jnp.float32)).astype(jnp.bfloat16)
    return [high, mid, low]


def all_sum(value, loss):
    dom, grp = lax.axis_size("dom"), lax.axis_size("grp")
    me_d, me_g = lax.axis_index("dom"), lax.axis_index("grp")
    bits_d, bits_g = dom.bit_length() - 1, grp.bit_length() - 1
    up = list(range(1, bits_d))
    stages = []
    if bits_d:
        stages.append(("dom", 0, 0))
    stages += [("dom", a, b) for a, b in zip(up, up[::-1])]
    stages += [("grp", bit, bit) for bit in range(bits_g)]
    odd = jnp.bitwise_and(me_d, 1)

    def send(block, axis, even_bit, odd_bit):
        count = lax.axis_size(axis)
        if even_bit == odd_bit:
            route = [(n, n ^ (1 << even_bit)) for n in range(count)]
        else:
            route = [(n, n ^ (1 << (odd_bit if n & 1 else even_bit))) for n in range(count)]
        return lax.ppermute(block, axis, route)

    def bit_of(axis, even_bit, odd_bit):
        me = me_d if axis == "dom" else me_g
        bit = jnp.where(odd == 1, odd_bit, even_bit)
        return jnp.bitwise_and(jnp.right_shift(me, bit), 1) == 1

    cols = value.shape[1]
    for axis, a, b in stages:
        half = value.shape[0] // 2
        upper = bit_of(axis, a, b)
        low, high = value[:half], value[half:]
        keep = jnp.where(upper, high, low)
        give = jnp.where(upper, low, high).astype(jnp.bfloat16)
        tail = jnp.stack([jnp.broadcast_to(p, (cols,)) for p in pieces(loss)])
        tail = jnp.pad(tail, ((0, 13), (0, 0)))
        came = send(jnp.concatenate([give, tail]), axis, a, b).astype(jnp.float32)
        value = keep + came[:half]
        loss = loss + (came[half, 0] + came[half + 1, 0] + came[half + 2, 0])
    value = value.astype(jnp.bfloat16)
    for axis, a, b in stages[::-1]:
        upper = bit_of(axis, a, b)
        came = send(value, axis, a, b)
        value = jnp.concatenate(
            [jnp.where(upper, came, value), jnp.where(upper, value, came)]
        )
    return value.astype(jnp.float32), loss


def body(embeddings, ada_state, relations, plan, src_rows, dst_rows, rel_ids):
    own_rows = embeddings[0]
    row_state = ada_state[0]
    rel_b = relations.astype(jnp.bfloat16)
    row_count, width = own_rows.shape
    loss_sum = jnp.zeros((), jnp.float32)
    rel_sum = jnp.zeros(relations.shape, jnp.float32)
    for round_no in range(ROUNDS):
        src_idx = src_rows[0, 0, round_no]
        dst_idx = dst_rows[0, 0, round_no]
        rel_idx = rel_ids[0, 0, round_no]
        own_b = own_rows.astype(jnp.bfloat16)
        payload = jnp.concatenate([own_b, encode((src_idx, dst_idx, rel_idx), width)])
        payload = exchange(payload, "dom", plan[round_no])
        src_b = own_b[src_idx]
        queries, onehot = project(src_b, rel_idx, rel_b)
        pair_b = payload[:row_count]
        pair_src, pair_dst, pair_rel = decode(payload[row_count:])
        edge_loss, deltas = score(queries, pair_b, dst_idx)
        dquery = jnp.dot(deltas, pair_b, preferred_element_type=jnp.float32).astype(jnp.bfloat16)
        pair_queries, _ = project(pair_b[pair_src], pair_rel, rel_b)
        _, pair_deltas = score(pair_queries, own_b, pair_dst)
        dblock = lax.dot_general(
            pair_deltas,
            pair_queries,
            (((0,), (0,)), ((), ())),
            preferred_element_type=jnp.float32,
        ).astype(jnp.bfloat16)
        back = jnp.einsum("ef,kdf->ked", dquery, rel_b, preferred_element_type=jnp.float32)
        src_grad = jnp.sum(onehot[:, :, None] * back, axis=0)
        gradient = jnp.zeros((row_count, width), jnp.float32).at[src_idx].add(src_grad)
        masked = (onehot[:, :, None] * dquery.astype(jnp.float32)).astype(jnp.bfloat16)
        rel_part = jnp.einsum("ed,kef->kdf", src_b, masked, preferred_element_type=jnp.float32)
        gradient = gradient + dblock.astype(jnp.float32)
        row_state = row_state + jnp.mean(gradient * gradient, axis=-1)
        own_rows = own_rows - LEARN_RATE * gradient / (jnp.sqrt(row_state)[:, None] + EPSILON)
        loss_sum = loss_sum + edge_loss
        rel_sum = rel_sum + rel_part
    rel_total, loss_total = all_sum(rel_sum.reshape(-1, width), loss_sum)
    mean_loss = loss_total / (lax.axis_size("dom") * lax.axis_size("grp") * ROUNDS * EDGES)
    return (own_rows[None], row_state[None], rel_total.reshape(relations.shape), mean_loss)


def solution(mesh):
    return jax.shard_map(
        body,
        mesh=mesh,
        in_specs=(
            P("grp", "dom", None),
            P("grp", "dom"),
            P(),
            P(),
            P("grp", "dom", None, None),
            P("grp", "dom", None, None),
            P("grp", "dom", None, None),
        ),
        out_specs=(P("grp", "dom", None), P("grp", "dom"), P(), P()),
        check_vma=False,
    )
```

```python
import functools
import math

import jax
import jax.numpy as jnp
from jax import lax
from jax.experimental import pallas as pl
from jax.experimental.pallas import tpu as pltpu
from jax.sharding import PartitionSpec as P

EDGES = 512
ROUNDS = 2


LEARN_RATE = 0.1
EPSILON = 1e-08
DIGIT = 3
RADIX_BITS = 7
PAD = 16
NT = (((1,), (1,)), ((), ()))
NN = (((1,), (0,)), ((), ()))
BF = jnp.bfloat16
F32 = jnp.float32
ROW_BLOCK = 16


def mm(a, b, dims=NN):
    return lax.dot_general(a, b, dims, preferred_element_type=F32)


def size_of(shape, dtype):
    return math.prod(shape) * jnp.dtype(dtype).itemsize


def call(kernel, outs, args, flops=0, name=None, room=0):
    moved = sum(size_of(a.shape, a.dtype) for a in args) + sum(size_of(*o) for o in outs)
    return pl.pallas_call(
        kernel,
        out_shape=[jax.ShapeDtypeStruct(s, d) for s, d in outs],
        in_specs=[pl.BlockSpec(memory_space=pltpu.VMEM)] * len(args),
        out_specs=[pl.BlockSpec(memory_space=pltpu.VMEM)] * len(outs),
        compiler_params=pltpu.CompilerParams(vmem_limit_bytes=moved + (1 << 20) + room),
        cost_estimate=pl.CostEstimate(flops=flops, bytes_accessed=moved, transcendentals=0),
        name=name,
    )(*args)


def put_rows(shape, rows):
    at = lax.broadcasted_iota(jnp.int32, shape, 0)
    out = jnp.zeros(shape, F32)
    for n, row in enumerate(rows):
        out = jnp.where(at == n, row, out)
    return out


def encoded(refs, round_no, width):
    rows = []
    for ref in refs:
        idx = ref[round_no : round_no + 1, :]
        rows.append(jnp.right_shift(idx, RADIX_BITS).astype(F32))
        rows.append(jnp.bitwise_and(idx, (1 << RADIX_BITS) - 1).astype(F32))
    return put_rows((PAD, width), rows).astype(BF)


def decoded(tail):
    tail = tail.astype(F32)
    scale = float(1 << RADIX_BITS)
    return [tail[2 * n : 2 * n + 1, :] * scale + tail[2 * n + 1 : 2 * n + 2, :] for n in range(3)]


def columns(rows):
    stacked = put_rows((8, rows[0].shape[1]), rows).T
    return [stacked[:, n : n + 1] for n in range(len(rows))]


def hit_cols(col, count):
    at = lax.broadcasted_iota(jnp.int32, (col.shape[0], count), 1).astype(F32)
    return at == col


def hit_rows(row, count):
    at = lax.broadcasted_iota(jnp.int32, (count, row.shape[1]), 0).astype(F32)
    return at == row


def picked(values, rel_col, k):
    return jnp.where(rel_col == k, values, jnp.zeros_like(values))


def project(src_b, rel_col, rel_ref):
    total = None
    for k in range(rel_ref.shape[0]):
        part = mm(picked(src_b, rel_col, k), rel_ref[k])
        total = part if total is None else total + part
    return total.astype(BF)


def own_edges(queries, pair_b, dst_col):
    scores = mm(queries, pair_b, NT)
    row_max = jnp.max(scores, axis=1, keepdims=True)
    exp_scores = jnp.exp(scores - row_max)
    row_total = jnp.sum(exp_scores, axis=1, keepdims=True)
    target = hit_cols(dst_col, pair_b.shape[0])
    aimed = jnp.sum(jnp.where(target, scores, 0.0), axis=1, keepdims=True)
    loss = jnp.sum(row_max + jnp.log(row_total) - aimed, axis=0, keepdims=True)
    deltas = (exp_scores / row_total - target.astype(F32)).astype(BF)
    return loss, mm(deltas, pair_b).astype(BF)


def pair_edges(own_b, pair_b, tail, rel_ref):
    src_row, dst_row, rel_row = decoded(tail)
    src_col, rel_col = columns([src_row, rel_row])
    rows = own_b.shape[0]
    src_b = mm(hit_cols(src_col, rows).astype(BF), pair_b).astype(BF)
    queries = project(src_b, rel_col, rel_ref)
    scores = mm(own_b, queries, NT)
    top = jnp.max(scores, axis=0, keepdims=True)
    exp_scores = jnp.exp(scores - top)
    total = jnp.sum(exp_scores, axis=0, keepdims=True)
    target = hit_rows(dst_row, rows).astype(F32)
    deltas = (exp_scores / total - target).astype(BF)
    return mm(deltas, queries).astype(BF).astype(F32)


def row_gradient(dquery, src_row, rel_col, rel_ref, rows):
    total = None
    for k in range(rel_ref.shape[0]):
        part = mm(picked(dquery, rel_col, k), rel_ref[k], NT)
        total = part if total is None else total + part
    return mm(hit_rows(src_row, rows).astype(BF), total.astype(BF))


def update(emb_ref, state_ref, gradient, new_ref, new_state_ref):
    rows = gradient.shape[0]
    mean = jnp.mean(gradient * gradient, axis=1, keepdims=True)
    (state,) = columns([state_ref[...]])
    state = state + mean
    scale = LEARN_RATE / (jnp.sqrt(state) + EPSILON)
    new_rows = emb_ref[...] - gradient * scale
    new_ref[...] = new_rows
    new_state_ref[...] = jnp.broadcast_to(state, (rows, 128)).T[0:1, :]
    return new_rows


def index_rows(refs, round_no):
    return [ref[round_no : round_no + 1, :].astype(F32) for ref in refs]


def pack_kernel(emb_ref, src_ref, dst_ref, rid_ref, out_ref):
    rows, width = emb_ref.shape
    out_ref[0:rows, :] = emb_ref[...].astype(BF)
    out_ref[rows : rows + PAD, :] = encoded((src_ref, dst_ref, rid_ref), 0, width)


def project_loop(src_b, rel_col, rel_ref):
    def step(k, total):
        return total + mm(picked(src_b, rel_col, k.astype(F32)), rel_ref[k])

    return lax.fori_loop(0, rel_ref.shape[0], step, jnp.zeros(src_b.shape, F32)).astype(BF)


def query_body(rows_b, src_ref, rid_ref, round_no, rel_ref, query_ref, src_t_ref):
    src_row, rel_row = index_rows((src_ref, rid_ref), round_no)
    src_col, rel_col = columns([src_row, rel_row])
    src_b = mm(hit_cols(src_col, rows_b.shape[0]).astype(BF), rows_b).astype(BF)
    query_ref[...] = project_loop(src_b, rel_col, rel_ref)
    src_t_ref[...] = src_b.T


def first_query_kernel(own_ref, rel_in_ref, src_ref, rid_ref, rel_ref, query_ref, src_t_ref):
    rel_ref[...] = rel_in_ref[...].astype(BF)
    rows = own_ref.shape[0] - PAD
    query_body(own_ref[0:rows, :], src_ref, rid_ref, 0, rel_ref, query_ref, src_t_ref)


def relation_part(src_t_ref, dquery, rel_col, k):
    return mm(src_t_ref[...], picked(dquery, rel_col, k))


def next_query_kernel(
    round_no, own_ref, rel_ref, src_ref, rid_ref, old_t_ref, dquery_ref, query_ref, src_t_ref, part_ref
):
    rows = own_ref.shape[0] - PAD
    query_body(own_ref[0:rows, :], src_ref, rid_ref, round_no, rel_ref, query_ref, src_t_ref)
    (rel_col,) = columns(index_rows((rid_ref,), round_no - 1))

    def step(k, carry):
        part_ref[k] = relation_part(old_t_ref, dquery_ref[...], rel_col, k.astype(F32))
        return carry

    lax.fori_loop(0, rel_ref.shape[0], step, 0)


def round_kernel(
    round_no,
    pair_ref,
    own_ref,
    emb_ref,
    state_ref,
    query_ref,
    rel_ref,
    src_ref,
    dst_ref,
    rid_ref,
    new_ref,
    next_ref,
    new_state_ref,
    dquery_ref,
    loss_ref,
):
    rows, width = emb_ref.shape
    pair_b = pair_ref[0:rows, :]
    src_row, dst_row, rel_row = index_rows((src_ref, dst_ref, rid_ref), round_no)
    dst_col, rel_col = columns([dst_row, rel_row])
    loss, dquery = own_edges(query_ref[...], pair_b, dst_col)
    loss_ref[...] = jnp.broadcast_to(loss, loss_ref.shape)
    dquery_ref[...] = dquery
    gradient = pair_edges(own_ref[0:rows, :], pair_b, pair_ref[rows : rows + PAD, :], rel_ref)
    gradient = gradient + row_gradient(dquery, src_row, rel_col, rel_ref, rows)
    new_rows = update(emb_ref, state_ref, gradient, new_ref, new_state_ref)
    next_ref[0:rows, :] = new_rows.astype(BF)
    next_ref[rows : rows + PAD, :] = encoded((src_ref, dst_ref, rid_ref), round_no + 1, width)


def last_own_kernel(
    round_no,
    stage,
    pair_ref,
    query_ref,
    src_t_ref,
    dst_ref,
    rid_ref,
    part_ref,
    old_loss_ref,
    dquery_ref,
    loss_ref,
    *give_refs,
):
    rows = pair_ref.shape[0] - PAD
    dst_col, rel_col = columns(index_rows((dst_ref, rid_ref), round_no))
    loss, dquery = own_edges(query_ref[...], pair_ref[0:rows, :], dst_col)
    dquery_ref[...] = dquery
    total = old_loss_ref[...] + loss
    loss_ref[...] = total
    upper = stage.upper()
    for n, give_ref in enumerate(give_refs):
        k = 2 * n + 1 - upper
        if n == 0:
            give_ref[0:PAD, :] = loss_tail(total)
            base = PAD
        else:
            base = 0
        part = relation_part(src_t_ref, dquery, rel_col, k.astype(F32)) + part_ref[k]
        give_ref[base : base + part.shape[0], :] = part.astype(BF)


def keep_kernel(round_no, stage, src_t_ref, dquery_ref, rid_ref, part_ref, *keep_refs):
    (rel_col,) = columns(index_rows((rid_ref,), round_no))
    upper = stage.upper()
    for n, keep_ref in enumerate(keep_refs):
        k = 2 * n + upper
        keep_ref[...] = (
            relation_part(src_t_ref, dquery_ref[...], rel_col, k.astype(F32)) + part_ref[k]
        )


def last_rows_kernel(
    round_no,
    pair_ref,
    own_ref,
    emb_ref,
    state_ref,
    dquery_ref,
    rel_ref,
    src_ref,
    rid_ref,
    new_ref,
    new_state_ref,
):
    rows = emb_ref.shape[0]
    src_row, rel_row = index_rows((src_ref, rid_ref), round_no)
    (rel_col,) = columns([rel_row])
    gradient = pair_edges(
        own_ref[0:rows, :], pair_ref[0:rows, :], pair_ref[rows : rows + PAD, :], rel_ref
    )
    gradient = gradient + row_gradient(dquery_ref[...], src_row, rel_col, rel_ref, rows)
    update(emb_ref, state_ref, gradient, new_ref, new_state_ref)


def loss_tail(total):
    total = total[0:1, :]
    high = total.astype(BF).astype(F32)
    rest = total - high
    mid = rest.astype(BF).astype(F32)
    return put_rows((PAD, total.shape[1]), [high, mid, rest - mid]).astype(BF)


def loss_of(tail):
    tail = tail.astype(F32)
    return (tail[0:1, :] + tail[1:2, :]) + tail[2:3, :]


def halve_kernel(with_loss, final, stage, came_ref, keep_ref, *refs):
    base = PAD if with_loss else 0
    if with_loss:
        loss_in, *refs = refs
    if final:
        give_ref, *refs = refs
    else:
        give_ref, next_ref, *refs = refs
    count = keep_ref.shape[0]
    half = count // 2
    if with_loss:
        (loss_out,) = refs
        total = loss_in[...] + loss_of(came_ref[0:PAD, :])
        loss_out[...] = total
        give_ref[0:PAD, :] = loss_tail(total)
    total = keep_ref[...] + came_ref[base : base + count, :].astype(F32)
    if final:
        give_ref[base : base + count, :] = total.astype(BF)
    else:
        upper = stage.upper() == 1
        next_ref[...] = jnp.where(upper, total[half:], total[:half])
        give_ref[base : base + half, :] = jnp.where(upper, total[:half], total[half:]).astype(BF)


def meet_kernel(with_loss, came_ref, mine_ref, *refs):
    base = PAD if with_loss else 0
    if with_loss:
        loss_in, out_ref, loss_out = refs
        loss_out[...] = loss_in[...] + loss_of(came_ref[0:PAD, :])
    else:
        (out_ref,) = refs
    count = out_ref.shape[0]
    total = came_ref[base : base + count, :].astype(F32) + mine_ref[base : base + count, :].astype(F32)
    out_ref[...] = total.astype(BF)


def join_kernel(stage, mine_ref, came_ref, out_ref):
    half = mine_ref.shape[0]
    upper = stage.upper() == 1
    mine, came = mine_ref[...], came_ref[...]
    out_ref[0:half, :] = jnp.where(upper, came, mine)
    out_ref[half : 2 * half, :] = jnp.where(upper, mine, came)


def spread_kernel(stage, *refs):
    out_ref = refs[-1]
    k = pl.program_id(0)
    upper = stage.upper()
    for n in range(len(refs) // 2):
        mine_ref, came_ref = refs[2 * n], refs[2 * n + 1]

        @pl.when(k == 2 * n + upper)
        def _(mine_ref=mine_ref):
            out_ref[0] = mine_ref[...].astype(F32)

        @pl.when(k == 2 * n + 1 - upper)
        def _(came_ref=came_ref):
            out_ref[0] = came_ref[...].astype(F32)


def xor_route(axis, mask):
    return [(low, low ^ mask) for low in range(lax.axis_size(axis))]


class Stage:
    def __init__(self, axis, even_bit, odd_bit):
        self.axis, self.even_bit, self.odd_bit = axis, even_bit, odd_bit
        self.route = [
            (n, n ^ (1 << (odd_bit if n & 1 else even_bit))) for n in range(lax.axis_size(axis))
        ]

    def upper(self):
        me = lax.axis_index(self.axis)
        even = jnp.bitwise_and(jnp.right_shift(me, self.even_bit), 1)
        if self.even_bit == self.odd_bit:
            return even
        odd = jnp.bitwise_and(jnp.right_shift(me, self.odd_bit), 1)
        return jnp.where(jnp.bitwise_and(me, 1) == 1, odd, even)

    def swap(self, block):
        return lax.ppermute(block, self.axis, self.route)


def make_stages():
    bits_d = lax.axis_size("dom").bit_length() - 1
    bits_g = lax.axis_size("grp").bit_length() - 1
    up = list(range(1, bits_d))
    stages = [Stage("dom", 0, 0)]
    stages += [Stage("dom", a, b) for a, b in zip(up, up[::-1])]
    stages += [Stage("grp", bit, bit) for bit in range(bits_g)]
    return stages


def halve(stage, came, keep, loss, final):
    with_loss = loss is not None
    count, width = keep.shape
    base = PAD if with_loss else 0
    sent = count if final else count // 2
    if sent % ROW_BLOCK:
        total = keep + came[base:].astype(F32)
        if with_loss:
            loss = loss + loss_of(came[:PAD])
        if final:
            give, rest = total.astype(BF), None
        else:
            upper = stage.upper() == 1
            give = jnp.where(upper, total[:sent], total[sent:]).astype(BF)
            rest = jnp.where(upper, total[sent:], total[:sent])
        if with_loss:
            give = jnp.concatenate([loss_tail(loss), give])
        return give, rest, loss
    outs = [((base + sent, width), BF)]
    if not final:
        outs.append(((sent, width), F32))
    args = [came, keep]
    if with_loss:
        outs.append((loss.shape, F32))
        args.append(loss)
    got = list(
        call(functools.partial(halve_kernel, with_loss, final, stage), outs, args, name="halve")
    )
    give = got.pop(0)
    rest = None if final else got.pop(0)
    return give, rest, (got.pop(0) if with_loss else None)


def meet(came, mine, loss):
    with_loss = loss is not None
    base = PAD if with_loss else 0
    count, width = mine.shape[0] - base, mine.shape[1]
    if count % ROW_BLOCK:
        total = (came[base:].astype(F32) + mine[base:].astype(F32)).astype(BF)
        return total, (loss + loss_of(came[:PAD]) if with_loss else None)
    outs, args = [((count, width), BF)], [came, mine]
    if with_loss:
        outs.append((loss.shape, F32))
        args.append(loss)
    got = call(functools.partial(meet_kernel, with_loss), outs, args, name="meet")
    return got[0], (got[1] if with_loss else None)


def join(stage, mine, came):
    half, width = mine.shape
    if half % ROW_BLOCK:
        upper = stage.upper() == 1
        return jnp.concatenate([jnp.where(upper, came, mine), jnp.where(upper, mine, came)])
    (out,) = call(
        functools.partial(join_kernel, stage), [((2 * half, width), BF)], [mine, came], name="join"
    )
    return out


def all_sum(stages, gives, keeps, loss):
    losses = [loss] + [None] * (len(gives) - 1)
    gives, keeps = list(gives), list(keeps)
    streams = range(len(gives))
    for at, stage in enumerate(stages[:-1]):
        final = at == len(stages) - 2
        for n in streams:
            came = stage.swap(gives[n])
            gives[n], keeps[n], losses[n] = halve(
                stages[at + 1], came, keeps[n], losses[n], final
            )
    values = [None] * len(gives)
    for n in streams:
        came = stages[-1].swap(gives[n])
        values[n], losses[n] = meet(came, gives[n], losses[n])
    for stage in stages[-2:0:-1]:
        for n in streams:
            came = stage.swap(values[n])
            values[n] = join(stage, values[n], came)
    pairs = []
    for n in streams:
        pairs += [values[n], stages[0].swap(values[n])]
    rows, width = values[0].shape
    count = 2 * len(gives)
    total = pl.pallas_call(
        functools.partial(spread_kernel, stages[0]),
        grid=(count,),
        out_shape=jax.ShapeDtypeStruct((count, rows, width), F32),
        in_specs=[pl.BlockSpec(memory_space=pltpu.VMEM)] * count,
        out_specs=pl.BlockSpec((1, rows, width), lambda k: (k, 0, 0)),
        compiler_params=pltpu.CompilerParams(vmem_limit_bytes=8 << 20),
        name="spread",
    )(*pairs)
    return total, losses[0][0, 0]


def exchange(block, axis, mask, beside):
    bits = lax.axis_size(axis).bit_length() - 1
    done = 0
    extra = None
    while done < bits:
        width = min(DIGIT, bits - done)
        digit = jnp.bitwise_and(jnp.right_shift(mask, done), (1 << width) - 1)
        last = done + width >= bits
        branches = []
        for value in range(1 << width):

            def branch(x, value=value, done=done, last=last):
                if value:
                    x = lax.ppermute(x, axis, xor_route(axis, value << done))
                return (x, beside()) if last else x

            if value or done or not last:
                branches.append(branch)
        if done == 0 and last:
            digit = digit - 1
        got = lax.switch(digit, branches, block)
        block, extra = got if last else (got, None)
        done += width
    return block, extra


def body(embeddings, ada_state, relations, plan, src_rows, dst_rows, rel_ids):
    rows, width = embeddings.shape[1:]
    count = relations.shape[0]
    edges = src_rows.shape[-1]
    emb = embeddings[0]
    src, dst, rid = src_rows[0, 0], dst_rows[0, 0], rel_ids[0, 0]
    square = 2 * rows * width * edges
    stages = make_stages()
    packed = ((rows + PAD, width), BF)
    edge_b = ((edges, width), BF)
    edge_t = ((width, edges), BF)
    part = (relations.shape, F32)
    line = ((8, width), F32)

    (own,) = call(pack_kernel, [packed], [emb, src, dst, rid], name="pack")
    pair, (rel_b, query, src_t) = exchange(
        own,
        "dom",
        plan[0],
        lambda: tuple(
            call(
                first_query_kernel,
                [(relations.shape, BF), edge_b, edge_t],
                [own, relations, src, rid],
                flops=5 * square,
                name="query",
                room=6 << 20,
            )
        ),
    )
    new, own_next, state, dquery, loss = call(
        functools.partial(round_kernel, 0),
        [((rows, width), F32), packed, ((1, rows), F32), edge_b, line],
        [pair, own, emb, ada_state, query, rel_b, src, dst, rid],
        flops=14 * square,
        name="round",
        room=12 << 20,
    )
    pair, (query, src_t, rel_part) = exchange(
        own_next,
        "dom",
        plan[1],
        lambda: tuple(
            call(
                functools.partial(next_query_kernel, 1),
                [edge_b, edge_t, part],
                [own_next, rel_b, src, rid, src_t, dquery],
                flops=9 * square,
                name="query",
                room=6 << 20,
            )
        ),
    )
    halves = count // 2
    dquery, loss, *gives = call(
        functools.partial(last_own_kernel, 1, stages[0]),
        [edge_b, line] + [((PAD + width, width), BF)] + [((width, width), BF)] * (halves - 1),
        [pair, query, src_t, dst, rid, rel_part, loss],
        flops=4 * square,
        name="own",
        room=8 << 20,
    )
    keeps = call(
        functools.partial(keep_kernel, 1, stages[0]),
        [((width, width), F32)] * halves,
        [src_t, dquery, rid, rel_part],
        flops=2 * square,
        name="keep",
        room=4 << 20,
    )
    new, state = call(
        functools.partial(last_rows_kernel, 1),
        [((rows, width), F32), ((1, rows), F32)],
        [pair, own_next, new, state, dquery, rel_b, src, rid],
        flops=12 * square,
        name="rows",
        room=10 << 20,
    )
    rel_total, loss_total = all_sum(stages, gives, keeps, loss)
    mean_loss = loss_total / (lax.axis_size("dom") * lax.axis_size("grp") * ROUNDS * EDGES)
    return (new[None], state, rel_total, mean_loss)


def solution(mesh):
    return jax.shard_map(
        body,
        mesh=mesh,
        in_specs=(
            P("grp", "dom", None),
            P("grp", "dom"),
            P(),
            P(),
            P("grp", "dom", None, None),
            P("grp", "dom", None, None),
            P("grp", "dom", None, None),
        ),
        out_specs=(P("grp", "dom", None), P("grp", "dom"), P(), P()),
        check_vma=False,
    )
```

```python
import functools
import math

import jax
import jax.numpy as jnp
from jax import lax
from jax.experimental import pallas as pl
from jax.experimental.pallas import tpu as pltpu
from jax.sharding import PartitionSpec as P


EDGES = 512
ROUNDS = 2


LEARN_RATE = 0.1
EPSILON = 1e-08
DIGIT = 3
RADIX_BITS = 7
PAD = 16


def ORDERS(over_d, back_d, over_g):
    return [(over_d + over_g, back_d + over_g), (over_g + over_d, over_g + back_d)]


SHARES = (3, 1)


NT = (((1,), (1,)), ((), ()))
NN = (((1,), (0,)), ((), ()))
BF = jnp.bfloat16
F32 = jnp.float32
ROW_BLOCK = 16


def mm(a, b, dims=NN):
    return lax.dot_general(a, b, dims, preferred_element_type=F32)


def size_of(shape, dtype):
    return math.prod(shape) * jnp.dtype(dtype).itemsize


class Fetched:
    def __init__(self, source, target, sems, first):
        self.target, self.shape = target, target.shape
        self.split = len(target.shape) == 3
        at = range(target.shape[0]) if self.split else [...]
        self.copies = [
            pltpu.make_async_copy(source.at[k], target.at[k], sems.at[first + n])
            for n, k in enumerate(at)
        ]
        for copy in self.copies:
            copy.start()

    def __getitem__(self, k):
        n = k if self.split else 0
        if self.copies[n] is not None:
            self.copies[n].wait()
            self.copies[n] = None
        return self.target[k]


def copies_of(shape):
    return shape[0] if len(shape) == 3 else 1


def call(kernel, outs, args, flops=0, room=0, fetch=()):
    arrays = [*args, *fetch]
    moved = sum(size_of(a.shape, a.dtype) for a in arrays) + sum(size_of(*o) for o in outs)

    def whole(*refs):
        first, rest = refs[: len(args)], refs[len(args) :]
        sources, rest = rest[: len(fetch)], rest[len(fetch) :]
        out_refs, rest = rest[: len(outs)], rest[len(outs) :]
        copies, used = [], 0
        for n, source in enumerate(sources):
            copies.append(Fetched(source, rest[n], rest[-1], used))
            used += copies_of(source.shape)
        kernel(*first, *copies, *out_refs)

    scratch = [pltpu.VMEM(a.shape, a.dtype) for a in fetch]
    if fetch:
        scratch.append(pltpu.SemaphoreType.DMA((sum(copies_of(a.shape) for a in fetch),)))
    return pl.pallas_call(
        whole,
        out_shape=[jax.ShapeDtypeStruct(s, d) for s, d in outs],
        in_specs=[pl.BlockSpec(memory_space=pltpu.VMEM)] * len(args)
        + [pl.BlockSpec(memory_space=pltpu.HBM)] * len(fetch),
        out_specs=[pl.BlockSpec(memory_space=pltpu.VMEM)] * len(outs),
        scratch_shapes=scratch,
        compiler_params=pltpu.CompilerParams(
            vmem_limit_bytes=None if room is None else moved + (1 << 20) + room
        ),
        cost_estimate=pl.CostEstimate(flops=flops, bytes_accessed=moved, transcendentals=0),
    )(*arrays)


def put_rows(shape, rows):
    at = lax.broadcasted_iota(jnp.int32, shape, 0)
    out = jnp.zeros(shape, F32)
    for n, row in enumerate(rows):
        out = jnp.where(at == n, row, out)
    return out


def encoded(refs, round_no, width):
    rows = []
    for ref in refs:
        idx = ref[round_no : round_no + 1, :]
        rows.append(jnp.right_shift(idx, RADIX_BITS).astype(F32))
        rows.append(jnp.bitwise_and(idx, (1 << RADIX_BITS) - 1).astype(F32))
    return put_rows((PAD, width), rows).astype(BF)


def decoded(tail):
    tail = tail.astype(F32)
    scale = float(1 << RADIX_BITS)
    return [tail[2 * n : 2 * n + 1, :] * scale + tail[2 * n + 1 : 2 * n + 2, :] for n in range(3)]


def columns(rows):
    stacked = put_rows((8, rows[0].shape[1]), rows).T
    return [stacked[:, n : n + 1] for n in range(len(rows))]


def hit_cols(col, count):
    at = lax.broadcasted_iota(jnp.int32, (col.shape[0], count), 1).astype(F32)
    return at == col


def hit_rows(row, count):
    at = lax.broadcasted_iota(jnp.int32, (count, row.shape[1]), 0).astype(F32)
    return at == row


def picked(values, rel_col, k):
    return jnp.where(rel_col == k, values, jnp.zeros_like(values))


def project(src_b, rel_col, rel_ref):
    total = None
    for k in range(rel_ref.shape[0]):
        part = mm(picked(src_b, rel_col, k), rel_ref[k])
        total = part if total is None else total + part
    return total.astype(BF)


def own_edges(queries, pair_b, dst_col):
    scores = mm(queries, pair_b, NT)
    row_max = jnp.max(scores, axis=1, keepdims=True)
    exp_scores = jnp.exp(scores - row_max)
    row_total = jnp.sum(exp_scores, axis=1, keepdims=True)
    target = hit_cols(dst_col, pair_b.shape[0])
    aimed = jnp.sum(jnp.where(target, scores, 0.0), axis=1, keepdims=True)
    loss = jnp.sum(row_max + jnp.log(row_total) - aimed, axis=0, keepdims=True)
    deltas = (exp_scores / row_total - target.astype(F32)).astype(BF)
    return loss, mm(deltas, pair_b).astype(BF)


def pair_queries(pair_b, tail, rel_ref):
    src_row, _, rel_row = decoded(tail)
    src_col, rel_col = columns([src_row, rel_row])
    src_b = mm(hit_cols(src_col, pair_b.shape[0]).astype(BF), pair_b).astype(BF)
    return project(src_b, rel_col, rel_ref)


def pair_block(own_b, queries, tail):
    _, dst_row, _ = decoded(tail)
    scores = mm(own_b, queries, NT)
    top = jnp.max(scores, axis=0, keepdims=True)
    exp_scores = jnp.exp(scores - top)
    total = jnp.sum(exp_scores, axis=0, keepdims=True)
    target = hit_rows(dst_row, own_b.shape[0]).astype(F32)
    deltas = (exp_scores / total - target).astype(BF)
    return mm(deltas, queries).astype(BF)


def back_project(dquery, rel_col, rel_ref):
    total = None
    for k in range(rel_ref.shape[0]):
        part = mm(picked(dquery, rel_col, k), rel_ref[k], NT)
        total = part if total is None else total + part
    return total.astype(BF)


def add_rows(back, src_row, rows):
    return mm(hit_rows(src_row, rows).astype(BF), back)


def update(emb_ref, state_ref, gradient, new_ref, new_state_ref):
    rows = gradient.shape[0]
    mean = jnp.mean(gradient * gradient, axis=1, keepdims=True)
    (state,) = columns([state_ref[...]])
    state = state + mean
    scale = LEARN_RATE / (jnp.sqrt(state) + EPSILON)
    new_rows = emb_ref[...] - gradient * scale
    new_ref[...] = new_rows
    new_state_ref[...] = jnp.broadcast_to(state, (rows, 128)).T[0:1, :]
    return new_rows


def index_rows(refs, round_no):
    return [ref[round_no : round_no + 1, :].astype(F32) for ref in refs]


def pack_kernel(emb, src, dst, rid, out_ref):
    width = out_ref.shape[1]
    rows = out_ref.shape[0] - PAD
    out_ref[rows : rows + PAD, :] = encoded([x[...] for x in (src, dst, rid)], 0, width)
    out_ref[0:rows, :] = emb[...].astype(BF)


def project_loop(src_b, rel_col, rel_ref):
    def step(k, total):
        return total + mm(picked(src_b, rel_col, k.astype(F32)), rel_ref[k])

    return lax.fori_loop(0, rel_ref.shape[0], step, jnp.zeros(src_b.shape, F32)).astype(BF)


def query_body(rows_b, src_ref, rid_ref, round_no, rel_ref, query_ref, src_t_ref):
    src_row, rel_row = index_rows((src_ref, rid_ref), round_no)
    src_col, rel_col = columns([src_row, rel_row])
    src_b = mm(hit_cols(src_col, rows_b.shape[0]).astype(BF), rows_b).astype(BF)
    query_ref[...] = project_loop(src_b, rel_col, rel_ref)
    src_t_ref[...] = src_b.T


def first_query_kernel(own_ref, rel_in_ref, src_ref, rid_ref, rel_ref, query_ref, src_t_ref):
    rel_ref[...] = rel_in_ref[...].astype(BF)
    rows = own_ref.shape[0] - PAD
    query_body(own_ref[0:rows, :], src_ref, rid_ref, 0, rel_ref, query_ref, src_t_ref)


def half_rows(ref, which):
    half = ref.shape[0] // 2
    return ref[pl.ds(pl.multiple_of(which * half, half), half), :]


def relation_part(src_half, dquery, rel_col, k):
    return mm(src_half, picked(dquery, rel_col, k))


def next_query_kernel(
    round_no,
    stage,
    own_ref,
    rel_ref,
    src_ref,
    rid_ref,
    old_t_ref,
    dquery_ref,
    query_ref,
    src_t_ref,
    give_ref,
    keep_ref,
):
    rows = own_ref.shape[0] - PAD
    query_body(own_ref[0:rows, :], src_ref, rid_ref, round_no, rel_ref, query_ref, src_t_ref)
    (rel_col,) = columns(index_rows((rid_ref,), round_no - 1))
    upper = stage.upper()
    for ref, which in ((give_ref, 1 - upper), (keep_ref, upper)):
        src_half = half_rows(old_t_ref, which)

        def step(k, carry, ref=ref, src_half=src_half):
            ref[k] = relation_part(src_half, dquery_ref[...], rel_col, k.astype(F32))
            return carry

        lax.fori_loop(0, ref.shape[0], step, 0)


def round_kernel(
    round_no,
    pair_ref,
    own_ref,
    emb_ref,
    state_ref,
    query_ref,
    src_ref,
    dst_ref,
    rid_ref,
    rel_ref,
    new_ref,
    next_ref,
    new_state_ref,
    dquery_ref,
    loss_ref,
):
    rows, width = emb_ref.shape
    pair_b = pair_ref[0:rows, :]
    src_row, dst_row, rel_row = index_rows((src_ref, dst_ref, rid_ref), round_no)
    dst_col, rel_col = columns([dst_row, rel_row])
    loss, dquery = own_edges(query_ref[...], pair_b, dst_col)
    loss_ref[...] = jnp.broadcast_to(loss, loss_ref.shape)
    dquery_ref[...] = dquery
    tail = pair_ref[rows : rows + PAD, :]
    block = pair_block(own_ref[0:rows, :], pair_queries(pair_b, tail, rel_ref), tail)
    back = back_project(dquery, rel_col, rel_ref)
    gradient = block.astype(F32) + add_rows(back, src_row, rows)
    new_rows = update(emb_ref, state_ref, gradient, new_ref, new_state_ref)
    next_ref[0:rows, :] = new_rows.astype(BF)
    next_ref[rows : rows + PAD, :] = encoded((src_ref, dst_ref, rid_ref), round_no + 1, width)


def last_own_kernel(
    round_no,
    stage,
    pair_ref,
    query_ref,
    src_t_ref,
    dst_ref,
    rid_ref,
    old_loss_ref,
    old,
    dquery_ref,
    loss_ref,
    *give_refs,
):
    rows = pair_ref.shape[0] - PAD
    dst_col, rel_col = columns(index_rows((dst_ref, rid_ref), round_no))
    loss, dquery = own_edges(query_ref[...], pair_ref[0:rows, :], dst_col)
    dquery_ref[...] = dquery
    total = old_loss_ref[...] + loss
    loss_ref[...] = total
    src_half = half_rows(src_t_ref, 1 - stage.upper())
    at = 0
    for n, give_ref in enumerate(give_refs):
        base = 0
        if n == len(give_refs) - 1:
            give_ref[0:PAD, :] = loss_tail(total)
            base = PAD
        half = src_half.shape[0]
        for j in range((give_ref.shape[0] - base) // half):
            part = relation_part(src_half, dquery, rel_col, at) + old[at]
            give_ref[base + j * half : base + (j + 1) * half, :] = part.astype(BF)
            at += 1


def keep_kernel(round_no, stage, src_t_ref, dquery_ref, rid_ref, part_ref, *keep_refs):
    (rel_col,) = columns(index_rows((rid_ref,), round_no))
    src_half = half_rows(src_t_ref, stage.upper())
    half = src_half.shape[0]
    at = 0
    for keep_ref in keep_refs:
        for j in range(keep_ref.shape[0] // half):
            part = relation_part(src_half, dquery_ref[...], rel_col, at) + part_ref[at]
            keep_ref[j * half : (j + 1) * half, :] = part
            at += 1


def pair_query_kernel(pair_ref, rel_ref, query_ref):
    rows = pair_ref.shape[0] - PAD
    query_ref[...] = pair_queries(pair_ref[0:rows, :], pair_ref[rows : rows + PAD, :], rel_ref)


def pair_block_kernel(pair_ref, own_ref, query_ref, block_ref):
    rows = own_ref.shape[0] - PAD
    tail = pair_ref[rows : rows + PAD, :]
    block_ref[...] = pair_block(own_ref[0:rows, :], query_ref[...], tail)


def back_kernel(round_no, dquery_ref, rid_ref, rel_ref, back_ref):
    (rel_col,) = columns(index_rows((rid_ref,), round_no))
    back_ref[...] = back_project(dquery_ref[...], rel_col, rel_ref)


def last_rows_kernel(
    round_no, emb_ref, state_ref, block_ref, back_ref, src_ref, new_ref, new_state_ref
):
    (src_row,) = index_rows((src_ref,), round_no)
    gradient = block_ref[...].astype(F32) + add_rows(back_ref[...], src_row, emb_ref.shape[0])
    update(emb_ref, state_ref, gradient, new_ref, new_state_ref)


def loss_tail(total):
    total = total[0:1, :]
    high = total.astype(BF).astype(F32)
    rest = total - high
    mid = rest.astype(BF).astype(F32)
    return put_rows((PAD, total.shape[1]), [high, mid, rest - mid]).astype(BF)


def loss_of(tail):
    tail = tail.astype(F32)
    return (tail[0:1, :] + tail[1:2, :]) + tail[2:3, :]


def halve_kernel(with_loss, final, stage, came_ref, keep_ref, *refs):
    base = PAD if with_loss else 0
    if with_loss:
        loss_in, *refs = refs
    if final:
        give_ref, *refs = refs
    else:
        give_ref, next_ref, *refs = refs
    count = keep_ref.shape[0]
    half = count // 2
    if with_loss:
        (loss_out,) = refs
        total = loss_in[...] + loss_of(came_ref[0:PAD, :])
        loss_out[...] = total
        give_ref[0:PAD, :] = loss_tail(total)
    total = keep_ref[...] + came_ref[base : base + count, :].astype(F32)
    if final:
        give_ref[base : base + count, :] = total.astype(BF)
    else:
        upper = stage.upper() == 1
        next_ref[...] = jnp.where(upper, total[half:], total[:half])
        give_ref[base : base + half, :] = jnp.where(upper, total[:half], total[half:]).astype(BF)


def meet_kernel(with_loss, came_ref, mine_ref, *refs):
    base = PAD if with_loss else 0
    if with_loss:
        loss_in, out_ref, loss_out = refs
        loss_out[...] = loss_in[...] + loss_of(came_ref[0:PAD, :])
    else:
        (out_ref,) = refs
    count = out_ref.shape[0]
    total = came_ref[base : base + count, :].astype(F32) + mine_ref[base : base + count, :].astype(F32)
    out_ref[...] = total.astype(BF)


def join_kernel(stage, mine_ref, came_ref, out_ref):
    half = mine_ref.shape[0]
    upper = stage.upper() == 1
    mine, came = mine_ref[...], came_ref[...]
    out_ref[0:half, :] = jnp.where(upper, came, mine)
    out_ref[half : 2 * half, :] = jnp.where(upper, mine, came)


def xor_route(axis, mask):
    return [(low, low ^ mask) for low in range(lax.axis_size(axis))]


class Stage:
    def __init__(self, even, odd):
        self.even, self.odd = even, odd
        count_d, count_g = lax.axis_size("dom"), lax.axis_size("grp")
        self.route = []
        for me_d in range(count_d):
            for me_g in range(count_g):
                axis, bit = odd if me_d & 1 else even
                to_d = me_d ^ (1 << bit if axis == "dom" else 0)
                to_g = me_g ^ (1 << bit if axis == "grp" else 0)
                self.route.append((me_d * count_g + me_g, to_d * count_g + to_g))

    def upper(self):
        def read(axis, bit):
            return jnp.bitwise_and(jnp.right_shift(lax.axis_index(axis), bit), 1)

        if self.even == self.odd:
            return read(*self.even)
        return jnp.where(read("dom", 0) == 1, read(*self.odd), read(*self.even))

    def swap(self, block):
        return lax.ppermute(block, ("dom", "grp"), self.route)


def bit_lists(bits_d, bits_g):
    return [("dom", bit) for bit in range(1, bits_d)], [("grp", bit) for bit in range(bits_g)]


def make_orders():
    over_d, over_g = bit_lists(
        lax.axis_size("dom").bit_length() - 1, lax.axis_size("grp").bit_length() - 1
    )
    back_d = over_d[::-1]
    orders = []
    for even, odd in ORDERS(over_d, back_d, over_g):
        orders.append([Stage(("dom", 0), ("dom", 0))] + [Stage(*pair) for pair in zip(even, odd)])
    return orders


def halve(stage, came, keep, loss, final):
    with_loss = loss is not None
    count, width = keep.shape
    base = PAD if with_loss else 0
    sent = count if final else count // 2
    if sent % ROW_BLOCK:
        total = keep + came[base:].astype(F32)
        if with_loss:
            loss = loss + loss_of(came[:PAD])
        if final:
            give, rest = total.astype(BF), None
        else:
            upper = stage.upper() == 1
            give = jnp.where(upper, total[:sent], total[sent:]).astype(BF)
            rest = jnp.where(upper, total[sent:], total[:sent])
        if with_loss:
            give = jnp.concatenate([loss_tail(loss), give])
        return give, rest, loss
    outs = [((base + sent, width), BF)]
    if not final:
        outs.append(((sent, width), F32))
    args = [came, keep]
    if with_loss:
        outs.append((loss.shape, F32))
        args.append(loss)
    got = list(call(functools.partial(halve_kernel, with_loss, final, stage), outs, args))
    give = got.pop(0)
    rest = None if final else got.pop(0)
    return give, rest, (got.pop(0) if with_loss else None)


def meet(came, mine, loss):
    with_loss = loss is not None
    base = PAD if with_loss else 0
    count, width = mine.shape[0] - base, mine.shape[1]
    if count % ROW_BLOCK:
        total = (came[base:].astype(F32) + mine[base:].astype(F32)).astype(BF)
        return total, (loss + loss_of(came[:PAD]) if with_loss else None)
    outs, args = [((count, width), BF)], [came, mine]
    if with_loss:
        outs.append((loss.shape, F32))
        args.append(loss)
    got = call(functools.partial(meet_kernel, with_loss), outs, args)
    return got[0], (got[1] if with_loss else None)


def join(stage, mine, came):
    half, width = mine.shape
    if half % ROW_BLOCK:
        upper = stage.upper() == 1
        return jnp.concatenate([jnp.where(upper, came, mine), jnp.where(upper, mine, came)])
    (out,) = call(functools.partial(join_kernel, stage), [((2 * half, width), BF)], [mine, came])
    return out


def all_sum(orders, gives, keeps, loss, shape):
    streams = range(len(gives))
    losses = [None] * (len(gives) - 1) + [loss]
    gives, keeps = list(gives), list(keeps)
    count = len(orders[0])
    for at in range(count - 1):
        for n in streams:
            came = orders[n][at].swap(gives[n])
            gives[n], keeps[n], losses[n] = halve(
                orders[n][at + 1], came, keeps[n], losses[n], at == count - 2
            )
    values = [None] * len(gives)
    for n in streams:
        came = orders[n][-1].swap(gives[n])
        values[n], losses[n] = meet(came, gives[n], losses[n])
    for at in range(count - 2, 0, -1):
        for n in streams:
            came = orders[n][at].swap(values[n])
            values[n] = join(orders[n][at], values[n], came)
    came = []
    for n in streams:
        came.append(orders[n][0].swap(values[n]))
    core = orders[0][0]
    total = spread(core, shape, values, None)
    total = spread(core, shape, came, total)
    return total, losses[-1][0, 0]


def spread_kernel(stage, flip, streams, *refs):
    value_refs, (out_ref, wide_ref, sems) = refs[:streams], refs[-3:]
    half = out_ref.shape[1] // 2
    which = 1 - stage.upper() if flip else stage.upper()
    rows = pl.ds(pl.multiple_of(which * half, half), half)
    at, copies = 0, []
    for value_ref in value_refs:
        for j in range(value_ref.shape[0] // half):
            wide_ref[at] = value_ref[j * half : (j + 1) * half, :].astype(F32)
            copies.append(
                pltpu.make_async_copy(wide_ref.at[at], out_ref.at[at, rows, :], sems.at[at])
            )
            copies[-1].start()
            at += 1
    for copy in copies:
        copy.wait()


def spread(stage, shape, values, total):
    known = [] if total is None else [total]
    count, rows, width = shape
    return pl.pallas_call(
        functools.partial(spread_kernel, stage, bool(known), len(values)),
        out_shape=jax.ShapeDtypeStruct(shape, F32),
        in_specs=[pl.BlockSpec(memory_space=pltpu.VMEM)] * len(values)
        + [pl.BlockSpec(memory_space=pltpu.HBM)] * len(known),
        out_specs=pl.BlockSpec(memory_space=pltpu.HBM),
        scratch_shapes=[
            pltpu.VMEM((count, rows // 2, width), F32),
            pltpu.SemaphoreType.DMA((count,)),
        ],
        input_output_aliases={len(values): 0} if known else {},
        compiler_params=pltpu.CompilerParams(vmem_limit_bytes=8 << 20),
        cost_estimate=pl.CostEstimate(flops=0, bytes_accessed=4 << 20, transcendentals=0),
        name="spread",
    )(*values, *known)


def exchange(block, axis, mask, beside):
    bits = lax.axis_size(axis).bit_length() - 1
    done = 0
    extra = None
    while done < bits:
        width = min(DIGIT, bits - done)
        digit = jnp.bitwise_and(jnp.right_shift(mask, done), (1 << width) - 1)
        last = done + width >= bits
        branches = []
        for value in range(1 << width):

            def branch(x, value=value, done=done, last=last):
                if value:
                    x = lax.ppermute(x, axis, xor_route(axis, value << done))
                return (x, beside()) if last else x

            if value or done or not last:
                branches.append(branch)
        if done == 0 and last:
            digit = digit - 1
        got = lax.switch(digit, branches, block)
        block, extra = got if last else (got, None)
        done += width
    return block, extra


def body(embeddings, ada_state, relations, plan, src_rows, dst_rows, rel_ids):
    rows, width = embeddings.shape[1:]
    count = relations.shape[0]
    edges = src_rows.shape[-1]
    emb = embeddings[0]
    src, dst, rid = src_rows[0, 0], dst_rows[0, 0], rel_ids[0, 0]
    square = 2 * rows * width * edges
    orders = make_orders()
    packed = ((rows + PAD, width), BF)
    edge_b = ((edges, width), BF)
    edge_t = ((width, edges), BF)
    half = width // 2
    part = ((count, half, width), F32)
    sizes = [count * share // 4 for share in SHARES]
    line = ((8, width), F32)

    (own,) = call(pack_kernel, [packed], [], room=None, fetch=[emb, src, dst, rid])
    pair, (rel_b, query, src_t) = exchange(
        own,
        "dom",
        plan[0],
        lambda: tuple(
            call(
                first_query_kernel,
                [(relations.shape, BF), edge_b, edge_t],
                [own, relations, src, rid],
                flops=5 * square,
                room=6 << 20,
            )
        ),
    )
    new, own_next, state, dquery, loss = call(
        functools.partial(round_kernel, 0),
        [((rows, width), F32), packed, ((1, rows), F32), edge_b, line],
        [pair, own, emb, ada_state, query, src, dst, rid],
        fetch=[rel_b],
        flops=14 * square,
        room=12 << 20,
    )
    pair, (query, src_t, give_part, keep_part) = exchange(
        own_next,
        "dom",
        plan[1],
        lambda: tuple(
            call(
                functools.partial(next_query_kernel, 1, orders[0][0]),
                [edge_b, edge_t, part, part],
                [own_next, rel_b, src, rid, src_t, dquery],
                flops=9 * square,
                room=6 << 20,
            )
        ),
    )
    dquery, loss, *gives = call(
        functools.partial(last_own_kernel, 1, orders[0][0]),
        [edge_b, line]
        + [
            ((size * half + (PAD if n == len(sizes) - 1 else 0), width), BF)
            for n, size in enumerate(sizes)
        ],
        [pair, query, src_t, dst, rid, loss],
        fetch=[give_part],
        flops=4 * square,
        room=8 << 20,
    )
    keeps = call(
        functools.partial(keep_kernel, 1, orders[0][0]),
        [((size * half, width), F32) for size in sizes],
        [src_t, dquery, rid, keep_part],
        flops=2 * square,
        room=4 << 20,
    )
    (pair_query,) = call(
        pair_query_kernel, [edge_b], [pair], flops=5 * square, room=6 << 20, fetch=[rel_b]
    )
    (back,) = call(
        functools.partial(back_kernel, 1),
        [edge_b],
        [dquery, rid],
        flops=4 * square,
        room=4 << 20,
        fetch=[rel_b],
    )
    (block,) = call(
        pair_block_kernel,
        [((rows, width), BF)],
        [pair, own_next, pair_query],
        flops=3 * square,
        room=6 << 20,
    )
    new, state = call(
        functools.partial(last_rows_kernel, 1),
        [((rows, width), F32), ((1, rows), F32)],
        [new, state, block, back, src],
        flops=2 * square,
        room=6 << 20,
    )
    rel_total, loss_total = all_sum(orders, gives, keeps, loss, relations.shape)
    mean_loss = loss_total / (lax.axis_size("dom") * lax.axis_size("grp") * ROUNDS * EDGES)
    return (new[None], state, rel_total, mean_loss)


def solution(mesh):
    return jax.shard_map(
        body,
        mesh=mesh,
        in_specs=(
            P("grp", "dom", None),
            P("grp", "dom"),
            P(),
            P(),
            P("grp", "dom", None, None),
            P("grp", "dom", None, None),
            P("grp", "dom", None, None),
        ),
        out_specs=(P("grp", "dom", None), P("grp", "dom"), P(), P()),
        check_vma=False,
    )
```
